256 devices in a mesh: row: 16 (over x_lo, z), col: 16 (over x_hi, y, core).
Axes of the slice: x: 4 (x_hi: 2, x_lo: 2; x = x_hi * 2 + x_lo), y: 4, z: 8, core: 2. Of those that a mesh axis runs over, the one named last changes fastest.
Arguments:
- tensor: bfloat16 [4096, 2048, 128], P('row', 'col'), may hold values from -96 to 96
- factor_a: float32 [4096, 128], P(('row', 'col')), may hold values from -4.5 to 4.5
- factor_b: float32 [2048, 128], P(('col', 'row')), may hold values from -4.5 to 4.5
- factor_c: float32 [128, 128], replicated, may hold values from -4.5 to 4.5
Outputs:
- new_a: float32 [4096, 128], P(('row', 'col'))
- new_b: float32 [2048, 128], P(('col', 'row'))
- new_c: float32 [128, 128], replicated
The draws below stay inside these ranges and needn't reach their ends.
All inputs are finite; a program needn't handle non-finite values.
Results may differ from the reference program's by a relative error of at most 0.01.
Values may be sent and summed in bfloat16 or wider, within the bound.
A program may use at most 128 MiB of HBM per device.

```python
import jax
import jax.numpy as jnp
from jax import lax

I_DEV = 256
K = 128
R = 128
STEPS = 2
I = 4096
J = 2048


def factor_draw(key, salt, row_count):
    folded = jax.random.fold_in(key, salt)
    key_values, key_spread = jax.random.split(folded)
    position = jnp.arange(row_count, dtype=jnp.float32) / (row_count - 1)
    spread = jnp.exp(jax.random.uniform(key_spread, (row_count, 1), jnp.float32, 0.0, 2.3025851))
    values = jnp.clip(jax.random.normal(key_values, (row_count, R), jnp.float32), -3.0, 3.0) * 0.05
    trend = jnp.exp(0.5493061 * position)
    return (values * spread * trend[:, None]).astype(jnp.float32)


def draw_factor_a(key, part):
    return factor_draw(key, 11, I)


def draw_factor_b(key, part):
    return factor_draw(key, 23, J)


def draw_factor_c(key, part):
    return factor_draw(key, 37, K)


def draw_tensor(key, part):
    folded = jax.random.fold_in(key, 7)
    key_values = jax.random.fold_in(folded, 0)
    values = jnp.clip(jax.random.normal(key_values, (I, J, K), jnp.float32), -6.0, 6.0) * 16.0
    return values.astype(jnp.bfloat16)


def setup_inputs(seed: int = 0) -> dict:
    seeds = jax.random.split(jax.random.key(seed), 5)
    tensor = draw_tensor(jax.random.fold_in(seeds[4], 71), 0)
    factor_a = draw_factor_a(jax.random.fold_in(seeds[4], 71), 0)
    factor_b = draw_factor_b(jax.random.fold_in(seeds[4], 71), 0)
    factor_c = draw_factor_c(jax.random.fold_in(seeds[4], 71), 0)
    return dict(tensor=tensor, factor_a=factor_a, factor_b=factor_b, factor_c=factor_c)


damping = 0.9
scaling = 0.25
epsilon = 1e-6


def column_squares(values16):
    return jnp.sum(jnp.square(values16.astype(jnp.float32)), axis=0)


def local_terms(block, tile_a, tile_b, c16):
    rows_i, rows_j, depth = block.shape
    a16 = tile_a.astype(jnp.bfloat16)
    b16 = tile_b.astype(jnp.bfloat16)
    rank = a16.shape[1]
    pairs = (a16.astype(jnp.float32)[:, None, :] * b16.astype(jnp.float32)[None, :, :]).astype(jnp.bfloat16)
    pairs = pairs.reshape(rows_i * rows_j, rank)
    model = jnp.dot(pairs, c16.T, preferred_element_type=jnp.float32)
    resid = (block.reshape(rows_i * rows_j, depth).astype(jnp.float32) - model).astype(jnp.bfloat16)
    along = jnp.dot(resid, c16, preferred_element_type=jnp.float32).reshape(rows_i, rows_j, rank)
    grad_a = jnp.sum(along * b16.astype(jnp.float32)[None, :, :], axis=1)
    grad_b = jnp.sum(along * a16.astype(jnp.float32)[:, None, :], axis=0)
    grad_c = lax.dot_general(resid, pairs, (((0,), (0,)), ((), ())), preferred_element_type=jnp.float32)
    return grad_a, grad_b, grad_c


def reference(tensor, factor_a, factor_b, factor_c):
    rows_i, rows_j, depth = tensor.shape
    rank = factor_a.shape[1]
    blocks = tensor.reshape(rows_i // I_DEV, I_DEV, rows_j, depth)
    current_a, current_b, current_c = factor_a, factor_b, factor_c
    for step in range(STEPS):
        c16 = current_c.astype(jnp.bfloat16)
        norm_a = column_squares(current_a.astype(jnp.bfloat16))
        norm_b = column_squares(current_b.astype(jnp.bfloat16))
        norm_c = column_squares(c16)
        step_a = scaling / (norm_b * norm_c + epsilon)
        step_b = scaling / (norm_a * norm_c + epsilon)
        step_c = scaling / (norm_a * norm_b + epsilon)
        a_blocks = current_a.reshape(rows_i // I_DEV, I_DEV, rank)
        fixed_b = current_b

        def one_block(carry, inputs):
            block, tile_a = inputs
            grad_a, grad_b, grad_c = local_terms(block, tile_a, fixed_b, c16)
            return (carry[0] + grad_b, carry[1] + grad_c), grad_a

        start = (jnp.zeros((rows_j, rank), jnp.float32), jnp.zeros((depth, rank), jnp.float32))
        (total_b, total_c), parts_a = lax.scan(one_block, start, (blocks, a_blocks))
        total_a = parts_a.reshape(rows_i, rank)
        current_a = damping * current_a + step_a * total_a
        current_b = damping * current_b + step_b * total_b
        current_c = damping * current_c + step_c * total_c
    return current_a, current_b, current_c
```

```python
import jax
import jax.numpy as jnp
from jax import lax
from jax.experimental import pallas as pl
from jax.experimental.pallas import tpu as pltpu
from jax.sharding import PartitionSpec as P

STEPS = 2
N = 16
damping = 0.9
scaling = 0.25
epsilon = 1e-06

MESH = pl.DeviceIdType.MESH
bf16, f32 = jnp.bfloat16, jnp.float32
GC_UNROLL = 64
Z_UNROLL = 64
CHUNKS = 8


def peer_copy(axis, peer, src, dst, ssem, rsem):
    return pltpu.make_async_remote_copy(
        src_ref=src, dst_ref=dst, send_sem=ssem, recv_sem=rsem, device_id={axis: peer}, device_id_type=MESH
    )


def send_all(axis, me, src_of, dst, ssem, rsem):
    def body(d, carry):
        p = lax.rem(me + d, N)
        peer_copy(axis, p, src_of(p), dst.at[me], ssem.at[p], rsem.at[me]).start()
        return carry

    lax.fori_loop(1, N, body, 0)


def recv_all(axis, me, dst, ssem, rsem):
    def body(d, carry):
        p = lax.rem(me + d, N)
        peer_copy(axis, p, dst.at[p], dst.at[p], ssem.at[p], rsem.at[p]).wait_recv()
        return carry

    lax.fori_loop(1, N, body, 0)


def drain_all(axis, me, src_of, dst, ssem, rsem):
    def body(d, carry):
        p = lax.rem(me + d, N)
        peer_copy(axis, p, src_of(p), dst.at[me], ssem.at[p], rsem.at[me]).wait_send()
        return carry

    lax.fori_loop(1, N, body, 0)


def split_dot(x16, g):
    hi = g.astype(bf16)
    lo = (g - hi.astype(f32)).astype(bf16)
    return jnp.dot(x16, hi, preferred_element_type=f32) + jnp.dot(x16, lo, preferred_element_type=f32)


def third_mode(tv, ta_t, tb_t):
    rows_i, rows_j, depth = tv.shape
    rank = tb_t.shape[0]
    unroll = GC_UNROLL

    def body(ib, acc):
        at = ta_t[ib]
        bt = tb_t[...]
        pairs = jnp.concatenate(
            [bt * jnp.broadcast_to(at[:, u : u + 1], (rank, rows_j)) for u in range(unroll)], axis=1
        )
        block = tv[pl.ds(ib * unroll, unroll)].reshape(unroll * rows_j, depth)
        return acc + jnp.dot(pairs, block, preferred_element_type=f32)

    return lax.fori_loop(0, rows_i // unroll, body, jnp.zeros((rank, depth), f32))


def first_modes(tv, ta32, tb32, c16, ga):
    rows_i, rows_j, depth = tv.shape
    rank = c16.shape[1]
    unroll = Z_UNROLL

    def body(ib, gb):
        b = tb32[...]
        block = tv[pl.ds(ib * unroll, unroll)].reshape(unroll * rows_j, depth)
        along = jnp.dot(block, c16[...], preferred_element_type=f32)
        rows = []
        for u in range(unroll):
            z = along[u * rows_j : (u + 1) * rows_j]
            rows.append(jnp.sum(z * b, axis=0, keepdims=True))
            gb = gb + z * ta32[pl.ds(ib * unroll + u, 1), :]
        ga[pl.ds(ib * unroll, unroll), :] = jnp.concatenate(rows, axis=0)
        return gb

    return lax.fori_loop(0, rows_i // unroll, body, jnp.zeros((rows_j, rank), f32))


def kernel(
    t_ref, a_ref, b_ref, c_ref, oa_ref, ob_ref, oc_ref,
    tv, ta, tb, ta32, tb32, ta_t, tb_t, c16, ga,
    a16, b16, sa, sb, ra, rb, na_s, nb_s, na_r, nb_r, c1s, c1r, c2s, c2r, c3s, c3r,
    tsem, ssem, rsem,
):
    row, col = lax.axis_index("row"), lax.axis_index("col")
    rows_i, rows_j, depth = tv.shape
    rank = tb_t.shape[0]
    part = rows_i // CHUNKS

    def chunk(i):
        view = pl.ds(i * part, part)
        return pltpu.make_async_copy(t_ref.at[view], tv.at[view], tsem.at[i])

    for i in range(CHUNKS):
        chunk(i).start()

    barrier = pltpu.get_barrier_semaphore()

    def greet(d, carry):
        pl.semaphore_signal(barrier, inc=1, device_id={"row": lax.rem(row + d, N)}, device_id_type=MESH)
        pl.semaphore_signal(barrier, inc=1, device_id={"col": lax.rem(col + d, N)}, device_id_type=MESH)
        return carry

    lax.fori_loop(1, N, greet, 0)

    own_a, own_b = a_ref[...], b_ref[...]
    own_c = c_ref[pl.ds(pl.multiple_of(col * 8, 8), 8), :]
    third = c_ref[...]
    sent = []

    def exchange(axis, kind, src_of, dst):
        me = row if axis == "row" else col
        args = (axis, me, src_of, dst, ssem.at[kind], rsem.at[kind])
        send_all(*args)
        sent.append(args)

    def arrive(axis, kind, dst):
        me = row if axis == "row" else col
        recv_all(axis, me, dst, ssem.at[kind], rsem.at[kind])

    def gather(step, own_a, own_b):
        a16[step] = own_a.astype(bf16)
        b16[step] = own_b.astype(bf16)
        ta[step, col] = own_a.astype(bf16)
        tb[step, row] = own_b.astype(bf16)
        exchange("col", step * 9 + 0, lambda p: a16.at[step], ta.at[step])
        exchange("row", step * 9 + 1, lambda p: b16.at[step], tb.at[step])

    pl.semaphore_wait(barrier, 2 * (N - 1))
    gather(0, own_a, own_b)

    for step in range(STEPS):
        k0 = step * 9
        arrive("col", k0 + 0, ta.at[step])
        arrive("row", k0 + 1, tb.at[step])
        at16 = ta[step].reshape(rows_i, rank)
        b_full = tb[step].astype(f32).reshape(rows_j, rank)
        bt16 = b_full.astype(bf16)
        a_full = at16.astype(f32)
        ta32[...] = a_full
        tb32[...] = b_full
        part_na = jnp.sum(a_full * a_full, axis=0, keepdims=True)
        part_nb = jnp.sum(b_full * b_full, axis=0, keepdims=True)
        na_s[step] = part_na
        nb_s[step] = part_nb
        na_r[step, row] = part_na
        nb_r[step, col] = part_nb
        exchange("row", k0 + 2, lambda p: na_s.at[step], na_r.at[step])
        exchange("col", k0 + 3, lambda p: nb_s.at[step], nb_r.at[step])

        flip_a = a_full.T
        flip_b = b_full.T.astype(bf16)
        tb_t[...] = flip_b
        for ib in range(rows_i // GC_UNROLL):
            lane = ib * GC_UNROLL
            half = flip_a[:, lane // 128 * 128 : lane // 128 * 128 + 128]
            if lane % 128:
                half = pltpu.roll(half, 128 - lane % 128, 1)
            ta_t[ib] = half.astype(bf16)
        gram_a = jnp.dot(flip_a.astype(bf16), at16, preferred_element_type=f32)
        gram_b = jnp.dot(flip_b, bt16, preferred_element_type=f32)

        if step == 0:
            for i in range(CHUNKS):
                chunk(i).wait()
        gc_t = third_mode(tv, ta_t, tb_t)
        if step:
            arrive("col", k0 - 9 + 8, c3r.at[step - 1])
            third = c3r[step - 1].reshape(depth, rank)
        third16 = third.astype(bf16)
        c16[...] = third16
        c32 = third16.astype(f32)
        gram_c = jnp.dot(c32.T.astype(bf16), third16, preferred_element_type=f32)
        norm_c = jnp.sum(c32 * c32, axis=0, keepdims=True)

        gc = gc_t.T - split_dot(third16, gram_a * gram_b)
        c1s[step] = gc.reshape(N, 8, rank)
        c1r[step, col] = c1s[step, col]
        exchange("col", k0 + 4, lambda p: c1s.at[step, p], c1r.at[step])

        gb = first_modes(tv, ta32, tb32, c16, ga)
        gb = gb - split_dot(bt16, gram_a * gram_c)
        grad_a = ga[...] - split_dot(at16, gram_b * gram_c)
        sa[step] = grad_a.astype(bf16).reshape(N, 16, rank)
        sb[step] = gb.reshape(N, 8, rank).astype(bf16)
        ra[step, col] = sa[step, col]
        rb[step, row] = sb[step, row]
        exchange("col", k0 + 5, lambda p: sa.at[step, p], ra.at[step])
        exchange("row", k0 + 6, lambda p: sb.at[step, p], rb.at[step])

        arrive("col", k0 + 4, c1r.at[step])
        piece = jnp.sum(c1r[step], axis=0)
        c2s[step] = piece
        c2r[step, row] = piece
        exchange("row", k0 + 7, lambda p: c2s.at[step], c2r.at[step])

        arrive("row", k0 + 2, na_r.at[step])
        arrive("col", k0 + 3, nb_r.at[step])
        norm_a = jnp.sum(na_r[step], axis=0)
        norm_b = jnp.sum(nb_r[step], axis=0)
        step_a = scaling / (norm_b * norm_c + epsilon)
        step_b = scaling / (norm_a * norm_c + epsilon)
        step_c = scaling / (norm_a * norm_b + epsilon)

        arrive("col", k0 + 5, ra.at[step])
        arrive("row", k0 + 6, rb.at[step])
        own_a = damping * own_a + step_a * jnp.sum(ra[step].astype(f32), axis=0)
        own_b = damping * own_b + step_b * jnp.sum(rb[step].astype(f32), axis=0)
        if step + 1 < STEPS:
            gather(step + 1, own_a, own_b)
        else:
            oa_ref[...] = own_a
            ob_ref[...] = own_b

        arrive("row", k0 + 7, c2r.at[step])
        own_c = damping * own_c + step_c * jnp.sum(c2r[step], axis=0)
        c3s[step] = own_c
        c3r[step, col] = own_c
        exchange("col", k0 + 8, lambda p: c3s.at[step], c3r.at[step])

    arrive("col", 9 * (STEPS - 1) + 8, c3r.at[STEPS - 1])
    oc_ref[...] = c3r[STEPS - 1].reshape(depth, rank)
    for args in sent:
        drain_all(*args)


def local(tensor, factor_a, factor_b, factor_c):
    rows_i, rows_j, depth = tensor.shape
    mine_a, rank = factor_a.shape
    mine_b = factor_b.shape[0]
    vmem = pl.BlockSpec(memory_space=pltpu.VMEM)
    V, S = pltpu.VMEM, STEPS
    return pl.pallas_call(
        kernel,
        out_shape=[jax.ShapeDtypeStruct(x.shape, f32) for x in (factor_a, factor_b, factor_c)],
        in_specs=[pl.BlockSpec(memory_space=pl.ANY), vmem, vmem, vmem],
        out_specs=[vmem, vmem, vmem],
        scratch_shapes=[
            V((rows_i, rows_j, depth), bf16),
            V((S, N, mine_a, rank), bf16),
            V((S, N, mine_b, rank), bf16),
            V((rows_i, rank), f32),
            V((rows_j, rank), f32),
            V((rows_i // GC_UNROLL, rank, 128), bf16),
            V((rank, rows_j), bf16),
            V((depth, rank), bf16),
            V((rows_i, rank), f32),
            V((S, mine_a, rank), bf16),
            V((S, mine_b, rank), bf16),
            V((S, N, mine_a, rank), bf16),
            V((S, N, mine_b, rank), bf16),
            V((S, N, mine_a, rank), bf16),
            V((S, N, mine_b, rank), bf16),
            V((S, 1, rank), f32),
            V((S, 1, rank), f32),
            V((S, N, 1, rank), f32),
            V((S, N, 1, rank), f32),
            V((S, N, 8, rank), f32),
            V((S, N, 8, rank), f32),
            V((S, 8, rank), f32),
            V((S, N, 8, rank), f32),
            V((S, 8, rank), f32),
            V((S, N, 8, rank), f32),
            pltpu.SemaphoreType.DMA((CHUNKS,)),
            pltpu.SemaphoreType.DMA((9 * S, N)),
            pltpu.SemaphoreType.DMA((9 * S, N)),
        ],
        compiler_params=pltpu.CompilerParams(collective_id=0, has_side_effects=True),
    )(tensor, factor_a, factor_b, factor_c)


def solution(mesh):
    return jax.shard_map(
        local,
        mesh=mesh,
        in_specs=(P("row", "col", None), P(("row", "col"), None), P(("col", "row"), None), P()),
        out_specs=(P(("row", "col"), None), P(("col", "row"), None), P()),
        check_vma=False,
    )
```

```python
import jax
import jax.numpy as jnp
from jax import lax
from jax.experimental import pallas as pl
from jax.experimental.pallas import tpu as pltpu
from jax.sharding import PartitionSpec as P

STEPS = 2
N = 16
Z = 8
Q = 32
damping = 0.9
scaling = 0.25
epsilon = 1e-06

MESH = pl.DeviceIdType.MESH
bf16, f32 = jnp.bfloat16, jnp.float32
UNROLL = 64
CHUNKS = 8


class Group:
    def __init__(self, size, me, device):
        self.size, self.me, self.device = size, me, device

    def each(self, act):
        def body(d, carry):
            act(lax.rem(self.me + d, self.size))
            return carry

        lax.fori_loop(1, self.size, body, 0)


def remote(group, peer, src, dst, ssem, rsem):
    return pltpu.make_async_remote_copy(
        src_ref=src, dst_ref=dst, send_sem=ssem, recv_sem=rsem, device_id=group.device(peer), device_id_type=MESH
    )


def split_dot(x16, g):
    hi = g.astype(bf16)
    lo = (g - hi.astype(f32)).astype(bf16)
    return jnp.dot(x16, hi, preferred_element_type=f32) + jnp.dot(x16, lo, preferred_element_type=f32)


def swap(tv, tt, base, count):
    for u in range(count):
        tt[base + u] = tv[base + u].T


def third_mode(tt, ta32, tb16):
    rows_i, depth, rows_j = tt.shape
    rank = ta32.shape[1]

    def body(ib, gc):
        block = tt[pl.ds(ib * UNROLL, UNROLL)].reshape(UNROLL * depth, rows_j)
        along = jnp.dot(block, tb16[...], preferred_element_type=f32)
        for u in range(UNROLL):
            gc = gc + along[u * depth : (u + 1) * depth] * ta32[pl.ds(ib * UNROLL + u, 1), :]
        return gc

    return lax.fori_loop(0, rows_i // UNROLL, body, jnp.zeros((depth, rank), f32))


def first_modes(tv, ta32, tb32, c16, ga):
    rows_i, rows_j, depth = tv.shape
    rank = c16.shape[1]

    def body(ib, gb):
        b = tb32[...]
        block = tv[pl.ds(ib * UNROLL, UNROLL)].reshape(UNROLL * rows_j, depth)
        along = jnp.dot(block, c16[...], preferred_element_type=f32)
        rows = []
        for u in range(UNROLL):
            z = along[u * rows_j : (u + 1) * rows_j]
            rows.append(jnp.sum(z * b, axis=0, keepdims=True))
            gb = gb + z * ta32[pl.ds(ib * UNROLL + u, 1), :]
        ga[pl.ds(ib * UNROLL, UNROLL), :] = jnp.concatenate(rows, axis=0)
        return gb

    return lax.fori_loop(0, rows_i // UNROLL, body, jnp.zeros((rows_j, rank), f32))


AG_A, AG_B, NORM_A, NORM_B, RS_A, RS_B = range(6)
PLANE_RS, PLANE_AG = range(2)


def kernel(
    t_ref, a_ref, b_ref, c_ref, oa_ref, ob_ref, oc_ref,
    tv, tt, ta, tb, ta32, tb32, tb16, c16, cq, ga,
    a16, b16, sa, sb, ra, rb, na_s, nb_s, na_r, nb_r, c1s, c1r, c2s, c2r, c3s, c3r,
    tsem, ssem, rsem, plane_ssem, plane_rsem, line_ssem, line_rsem,
):
    row, col = lax.axis_index("row"), lax.axis_index("col")
    x_lo, z = lax.div(row, Z), lax.rem(row, Z)
    q = x_lo * N + col
    rows_i, rows_j, depth = tv.shape
    rank = c16.shape[1]
    part = rows_i // CHUNKS
    rows = Group(N, row, lambda p: (p, col))
    cols = Group(N, col, lambda p: (row, p))
    plane = Group(Q, q, lambda p: (lax.div(p, N) * Z + z, lax.rem(p, N)))
    line = Group(Z, z, lambda p: (x_lo * Z + p, col))

    def chunk(i):
        view = pl.ds(i * part, part)
        return pltpu.make_async_copy(t_ref.at[view], tv.at[view], tsem.at[i])

    for i in range(CHUNKS):
        chunk(i).start()

    barrier = pltpu.get_barrier_semaphore()

    def greet(group):
        group.each(
            lambda p: pl.semaphore_signal(barrier, inc=1, device_id=group.device(p), device_id_type=MESH)
        )

    greet(rows)
    greet(plane)

    sent = []

    def others(group, dst, ss, rs):
        view = dst.at[pl.ds(0, group.size - 1)]
        return remote(group, group.me, view, view, ss, rs)

    def send(group, src_of, dst, ss, rs):
        group.each(lambda p: remote(group, p, src_of(p), dst.at[group.me], ss, rs).start())
        sent.append((group, dst, ss, rs))

    def arrive(group, dst, ss, rs):
        others(group, dst, ss, rs).wait_recv()

    def sems(step, kind):
        return ssem.at[step * 6 + kind], rsem.at[step * 6 + kind]

    def plane_sems(step, kind):
        return plane_ssem.at[step * 2 + kind], plane_rsem.at[step * 2 + kind]

    def line_sems(step):
        return line_ssem.at[step], line_rsem.at[step]

    def gather_factors(step, own_a, own_b):
        b16[step] = own_b.astype(bf16)
        a16[step] = own_a.astype(bf16)
        send(rows, lambda p: b16.at[step], tb.at[step], *sems(step, AG_B))
        send(cols, lambda p: a16.at[step], ta.at[step], *sems(step, AG_A))
        tb[step, row] = own_b.astype(bf16)
        ta[step, col] = own_a.astype(bf16)

    def take_third(third):
        third16 = third.astype(bf16)
        c16[...] = third16
        c32 = third16.astype(f32)
        gram = jnp.dot(c32.T.astype(bf16), third16, preferred_element_type=f32)
        return third16, gram, jnp.sum(c32 * c32, axis=0, keepdims=True)

    def take_factors(step):
        arrive(cols, ta.at[step], *sems(step, AG_A))
        arrive(rows, tb.at[step], *sems(step, AG_B))
        a_full = ta[step].reshape(rows_i, rank).astype(f32)
        b_full = tb[step].astype(f32).reshape(rows_j, rank)
        ta32[...] = a_full
        tb32[...] = b_full
        tb16[...] = b_full.astype(bf16)
        part_na = jnp.sum(a_full * a_full, axis=0, keepdims=True)
        part_nb = jnp.sum(b_full * b_full, axis=0, keepdims=True)
        na_s[step] = part_na
        nb_s[step] = part_nb
        na_r[step, row] = part_na
        nb_r[step, col] = part_nb
        send(rows, lambda p: na_s.at[step], na_r.at[step], *sems(step, NORM_A))
        send(cols, lambda p: nb_s.at[step], nb_r.at[step], *sems(step, NORM_B))

    def grams(step):
        gram_a = jnp.dot(ta32[...].T.astype(bf16), ta[step].reshape(rows_i, rank), preferred_element_type=f32)
        gram_b = jnp.dot(tb32[...].T.astype(bf16), tb16[...], preferred_element_type=f32)
        return gram_a, gram_b

    def do_first_modes(step, gram_a, gram_b, gram_c):
        gb = first_modes(tv, ta32, tb32, c16, ga)
        gb = gb - split_dot(tb16[...], gram_a * gram_c)
        grad_a = ga[...] - split_dot(ta[step].reshape(rows_i, rank), gram_b * gram_c)
        sb[step] = gb.reshape(N, 8, rank).astype(bf16)
        sa[step] = grad_a.astype(bf16).reshape(N, 16, rank)
        send(rows, lambda p: sb.at[step, p], rb.at[step], *sems(step, RS_B))
        send(cols, lambda p: sa.at[step, p], ra.at[step], *sems(step, RS_A))
        rb[step, row] = sb[step, row]
        ra[step, col] = sa[step, col]

    def scatter_third(step, gc, third16, gram_a, gram_b):
        gc = gc - split_dot(third16, gram_a * gram_b)
        c1s[step] = gc.reshape(Q, 4, rank)
        send(plane, lambda p: c1s.at[step, p], c1r.at[step], *plane_sems(step, PLANE_RS))
        c1r[step, q] = c1s[step, q]

    def line_third(step):
        arrive(plane, c1r.at[step], *plane_sems(step, PLANE_RS))
        piece = jnp.sum(c1r[step], axis=0)
        c2s[step] = piece
        send(line, lambda p: c2s.at[step], c2r.at[step], *line_sems(step))
        c2r[step, z] = piece

    def gather_third(step, own_c, step_c):
        arrive(line, c2r.at[step], *line_sems(step))
        own_c = damping * own_c + step_c * jnp.sum(c2r[step], axis=0)
        c3s[step] = own_c
        send(plane, lambda p: c3s.at[step], c3r.at[step], *plane_sems(step, PLANE_AG))
        c3r[step, q] = own_c
        return own_c

    def whole_third(step):
        arrive(plane, c3r.at[step], *plane_sems(step, PLANE_AG))
        return c3r[step].reshape(depth, rank)

    def sizes(step, norm_c):
        arrive(rows, na_r.at[step], *sems(step, NORM_A))
        arrive(cols, nb_r.at[step], *sems(step, NORM_B))
        norm_a = jnp.sum(na_r[step], axis=0)
        norm_b = jnp.sum(nb_r[step], axis=0)
        return (
            scaling / (norm_b * norm_c + epsilon),
            scaling / (norm_a * norm_c + epsilon),
            scaling / (norm_a * norm_b + epsilon),
        )

    def update_first(step, own_a, own_b, step_a, step_b):
        arrive(rows, rb.at[step], *sems(step, RS_B))
        arrive(cols, ra.at[step], *sems(step, RS_A))
        own_a = damping * own_a + step_a * jnp.sum(ra[step].astype(f32), axis=0)
        own_b = damping * own_b + step_b * jnp.sum(rb[step].astype(f32), axis=0)
        return own_a, own_b

    own_a, own_b = a_ref[...], b_ref[...]
    third16, gram_c, norm_c = take_third(c_ref[...])
    cq[...] = c_ref[...].reshape(Q, 4, rank)
    own_c = cq[q]
    pl.semaphore_wait(barrier, N - 1 + Q - 1)
    gather_factors(0, own_a, own_b)

    def turn(i, carry):
        chunk(i).wait()
        swap(tv, tt, i * part, part)
        return carry

    lax.fori_loop(0, CHUNKS, turn, 0)

    take_factors(0)
    gram_a, gram_b = grams(0)
    do_first_modes(0, gram_a, gram_b, gram_c)
    gc = third_mode(tt, ta32, tb16)
    scatter_third(0, gc, third16, gram_a, gram_b)
    step_a, step_b, step_c = sizes(0, norm_c)
    own_a, own_b = update_first(0, own_a, own_b, step_a, step_b)
    gather_factors(1, own_a, own_b)
    line_third(0)

    take_factors(1)
    gram_a, gram_b = grams(1)
    own_c = gather_third(0, own_c, step_c)
    gc = third_mode(tt, ta32, tb16)
    third16, gram_c, norm_c = take_third(whole_third(0))
    scatter_third(1, gc, third16, gram_a, gram_b)
    do_first_modes(1, gram_a, gram_b, gram_c)
    line_third(1)
    step_a, step_b, step_c = sizes(1, norm_c)
    own_a, own_b = update_first(1, own_a, own_b, step_a, step_b)
    oa_ref[...] = own_a
    ob_ref[...] = own_b
    gather_third(1, own_c, step_c)
    oc_ref[...] = whole_third(1)

    for group, dst, ss, rs in sent:
        others(group, dst, ss, rs).wait_send()


def hand_over(a_ref, b_ref, c_ref, oa_ref, ob_ref, oc_ref):
    oa_ref[...] = a_ref[...]
    ob_ref[...] = b_ref[...]
    oc_ref[...] = c_ref[...]


def local(tensor, factor_a, factor_b, factor_c):
    rows_i, rows_j, depth = tensor.shape
    mine_a, rank = factor_a.shape
    mine_b = factor_b.shape[0]
    vmem = pl.BlockSpec(memory_space=pltpu.VMEM)
    V, S, D = pltpu.VMEM, STEPS, pltpu.SemaphoreType.DMA
    outs = pl.pallas_call(
        kernel,
        out_shape=[jax.ShapeDtypeStruct(x.shape, f32) for x in (factor_a, factor_b, factor_c)],
        in_specs=[pl.BlockSpec(memory_space=pl.ANY), vmem, vmem, vmem],
        out_specs=[vmem, vmem, vmem],
        scratch_shapes=[
            V((rows_i, rows_j, depth), bf16),
            V((rows_i, depth, rows_j), bf16),
            V((S, N, mine_a, rank), bf16),
            V((S, N, mine_b, rank), bf16),
            V((rows_i, rank), f32),
            V((rows_j, rank), f32),
            V((rows_j, rank), bf16),
            V((depth, rank), bf16),
            V((Q, 4, rank), f32),
            V((rows_i, rank), f32),
            V((S, mine_a, rank), bf16),
            V((S, mine_b, rank), bf16),
            V((S, N, mine_a, rank), bf16),
            V((S, N, mine_b, rank), bf16),
            V((S, N, mine_a, rank), bf16),
            V((S, N, mine_b, rank), bf16),
            V((S, 1, rank), f32),
            V((S, 1, rank), f32),
            V((S, N, 1, rank), f32),
            V((S, N, 1, rank), f32),
            V((S, Q, 4, rank), f32),
            V((S, Q, 4, rank), f32),
            V((S, 4, rank), f32),
            V((S, Z, 4, rank), f32),
            V((S, 4, rank), f32),
            V((S, Q, 4, rank), f32),
            D((CHUNKS,)),
            D((6 * S,)),
            D((6 * S,)),
            D((2 * S,)),
            D((2 * S,)),
            D((S,)),
            D((S,)),
        ],
        compiler_params=pltpu.CompilerParams(collective_id=0, has_side_effects=True),
    )(tensor, factor_a, factor_b, factor_c)
    return pl.pallas_call(
        hand_over,
        out_shape=[jax.ShapeDtypeStruct(x.shape, f32) for x in (factor_a, factor_b, factor_c)],
        in_specs=[vmem, vmem, vmem],
        out_specs=[vmem, vmem, vmem],
    )(*outs)


def solution(mesh):
    return jax.shard_map(
        local,
        mesh=mesh,
        in_specs=(P("row", "col", None), P(("row", "col"), None), P(("col", "row"), None), P()),
        out_specs=(P(("row", "col"), None), P(("col", "row"), None), P()),
        check_vma=False,
    )
```

```python
import jax
import jax.numpy as jnp
from jax import lax
from jax.experimental import pallas as pl
from jax.experimental.pallas import tpu as pltpu
from jax.sharding import PartitionSpec as P

STEPS = 2
N = 16
Z = 8
Q = 32
damping = 0.9
scaling = 0.25
epsilon = 1e-06

MESH = pl.DeviceIdType.MESH
bf16, f32 = jnp.bfloat16, jnp.float32
UNROLL = 128
CHUNKS = 8


class Group:
    def __init__(self, size, me, device, ring, unit):
        self.size, self.me, self.device = size, me, device
        near = lambda d: min(d // unit % ring, -(d // unit) % ring)
        self.offsets = sorted(range(1, size), key=lambda d: -near(d))

    def each(self, act):
        for d in self.offsets:
            act(lax.rem(self.me + d, self.size))


def remote(group, peer, src, dst, ssem, rsem):
    return pltpu.make_async_remote_copy(
        src_ref=src, dst_ref=dst, send_sem=ssem, recv_sem=rsem, device_id=group.device(peer), device_id_type=MESH
    )


def split(g):
    hi = g.astype(bf16)
    return hi, (g - hi.astype(f32)).astype(bf16)


def split_dot(x16, parts):
    hi, lo = parts
    return jnp.dot(x16, hi, preferred_element_type=f32) + jnp.dot(x16, lo, preferred_element_type=f32)


def swap(tv, tt, base, count):
    for u in range(count):
        tt[base + u] = tv[base + u].T


def third_mode(tt, ta32, tb16):
    rows_i, depth, rows_j = tt.shape
    rank = ta32.shape[1]

    def body(ib, gc):
        block = tt[pl.ds(ib * UNROLL, UNROLL)].reshape(UNROLL * depth, rows_j)
        along = jnp.dot(block, tb16[...], preferred_element_type=f32)
        for u in range(UNROLL):
            gc = gc + along[u * depth : (u + 1) * depth] * ta32[pl.ds(ib * UNROLL + u, 1), :]
        return gc

    return lax.fori_loop(0, rows_i // UNROLL, body, jnp.zeros((depth, rank), f32))


def first_modes(tv, ta32, tb32, c16, ga):
    rows_i, rows_j, depth = tv.shape
    rank = c16.shape[1]

    def body(ib, gb):
        b = tb32[...]
        block = tv[pl.ds(ib * UNROLL, UNROLL)].reshape(UNROLL * rows_j, depth)
        along = jnp.dot(block, c16[...], preferred_element_type=f32)
        rows = []
        for u in range(UNROLL):
            z = along[u * rows_j : (u + 1) * rows_j]
            rows.append(jnp.sum(z * b, axis=0, keepdims=True))
            gb = gb + z * ta32[pl.ds(ib * UNROLL + u, 1), :]
        ga[pl.ds(ib * UNROLL, UNROLL), :] = jnp.concatenate(rows, axis=0)
        return gb

    return lax.fori_loop(0, rows_i // UNROLL, body, jnp.zeros((rows_j, rank), f32))


AG_A, AG_B, NORM_A, NORM_B, RS_A, RS_B = range(6)
PLANE_RS, PLANE_AG = range(2)


def kernel(
    t_ref, a_ref, b_ref, c_ref, oa_ref, ob_ref, oc_ref,
    tv, tt, ta, tb, ta32, tb32, tb16, c16, cq, ga,
    a16, b16, sa, sb, ra, rb, na_s, nb_s, na_r, nb_r, c1s, c1r, c2s, c2r, c3s, c3r,
    tsem, ssem, rsem, plane_ssem, plane_rsem, line_ssem, line_rsem,
):
    row, col = lax.axis_index("row"), lax.axis_index("col")
    x_lo, z = lax.div(row, Z), lax.rem(row, Z)
    q = x_lo * N + col
    rows_i, rows_j, depth = tv.shape
    rank = c16.shape[1]
    part = rows_i // CHUNKS
    rows = Group(N, row, lambda p: (p, col), Z, 1)
    cols = Group(N, col, lambda p: (row, p), 4, 2)
    plane = Group(Q, q, lambda p: (lax.div(p, N) * Z + z, lax.rem(p, N)), 4, 2)
    line = Group(Z, z, lambda p: (x_lo * Z + p, col), Z, 1)

    def chunk(i):
        view = pl.ds(i * part, part)
        return pltpu.make_async_copy(t_ref.at[view], tv.at[view], tsem.at[i])

    for i in range(CHUNKS):
        chunk(i).start()

    barrier = pltpu.get_barrier_semaphore()

    def greet(group):
        group.each(
            lambda p: pl.semaphore_signal(barrier, inc=1, device_id=group.device(p), device_id_type=MESH)
        )

    greet(rows)
    greet(plane)

    sent = []

    def others(group, dst, ss, rs):
        view = dst.at[pl.ds(0, group.size - 1)]
        return remote(group, group.me, view, view, ss, rs)

    def send(group, src_of, dst, ss, rs):
        group.each(lambda p: remote(group, p, src_of(p), dst.at[group.me], ss, rs).start())
        sent.append((group, dst, ss, rs))

    def arrive(group, dst, ss, rs):
        others(group, dst, ss, rs).wait_recv()

    def sems(step, kind):
        return ssem.at[step * 6 + kind], rsem.at[step * 6 + kind]

    def plane_sems(step, kind):
        return plane_ssem.at[step * 2 + kind], plane_rsem.at[step * 2 + kind]

    def line_sems(step):
        return line_ssem.at[step], line_rsem.at[step]

    def gather_factors(step, own_a, own_b):
        b16[step] = own_b.astype(bf16)
        a16[step] = own_a.astype(bf16)
        send(rows, lambda p: b16.at[step], tb.at[step], *sems(step, AG_B))
        send(cols, lambda p: a16.at[step], ta.at[step], *sems(step, AG_A))
        tb[step, row] = own_b.astype(bf16)
        ta[step, col] = own_a.astype(bf16)

    def take_third(third16):
        c16[...] = third16
        c32 = third16.astype(f32)
        gram = jnp.dot(c32.T.astype(bf16), third16, preferred_element_type=f32)
        return gram, jnp.sum(c32 * c32, axis=0, keepdims=True)

    def take_factors(step):
        arrive(cols, ta.at[step], *sems(step, AG_A))
        arrive(rows, tb.at[step], *sems(step, AG_B))
        a_full = ta[step].reshape(rows_i, rank).astype(f32)
        b_full = tb[step].astype(f32).reshape(rows_j, rank)
        ta32[...] = a_full
        tb32[...] = b_full
        tb16[...] = b_full.astype(bf16)

    def send_norms(step):
        a_full, b_full = ta32[...], tb32[...]
        part_na = jnp.sum(a_full * a_full, axis=0, keepdims=True)
        part_nb = jnp.sum(b_full * b_full, axis=0, keepdims=True)
        na_s[step] = part_na
        nb_s[step] = part_nb
        na_r[step, row] = part_na
        nb_r[step, col] = part_nb
        send(rows, lambda p: na_s.at[step], na_r.at[step], *sems(step, NORM_A))
        send(cols, lambda p: nb_s.at[step], nb_r.at[step], *sems(step, NORM_B))

    def grams(step):
        gram_a = jnp.dot(ta32[...].T.astype(bf16), ta[step].reshape(rows_i, rank), preferred_element_type=f32)
        gram_b = jnp.dot(tb32[...].T.astype(bf16), tb16[...], preferred_element_type=f32)
        return gram_a, gram_b

    def do_first_modes(step, gram_a, gram_b, gram_c):
        gb = first_modes(tv, ta32, tb32, c16, ga)
        gb = gb - split_dot(tb16[...], split(gram_a * gram_c))
        grad_a = ga[...] - split_dot(ta[step].reshape(rows_i, rank), split(gram_b * gram_c))
        sb[step] = gb.reshape(N, 8, rank).astype(bf16)
        sa[step] = grad_a.astype(bf16).reshape(N, 16, rank)
        send(rows, lambda p: sb.at[step, p], rb.at[step], *sems(step, RS_B))
        send(cols, lambda p: sa.at[step, p], ra.at[step], *sems(step, RS_A))
        rb[step, row] = sb[step, row]
        ra[step, col] = sa[step, col]

    def scatter_third(step, gc, third16, gram_ab):
        gc = gc - split_dot(third16, gram_ab)
        c1s[step] = gc.reshape(Q, 4, rank)
        send(plane, lambda p: c1s.at[step, p], c1r.at[step], *plane_sems(step, PLANE_RS))
        c1r[step, q] = c1s[step, q]

    def line_third(step):
        arrive(plane, c1r.at[step], *plane_sems(step, PLANE_RS))
        piece = jnp.sum(c1r[step], axis=0)
        c2s[step] = piece
        send(line, lambda p: c2s.at[step], c2r.at[step], *line_sems(step))
        c2r[step, z] = piece

    def gather_third(step, own_c, step_c):
        arrive(line, c2r.at[step], *line_sems(step))
        own_c = damping * own_c + step_c * jnp.sum(c2r[step], axis=0)
        c3s[step] = own_c
        send(plane, lambda p: c3s.at[step], c3r.at[step], *plane_sems(step, PLANE_AG))
        c3r[step, q] = own_c
        return own_c

    def whole_third(step):
        arrive(plane, c3r.at[step], *plane_sems(step, PLANE_AG))
        return c3r[step].reshape(depth, rank)

    def sizes(step, norm_c):
        arrive(rows, na_r.at[step], *sems(step, NORM_A))
        arrive(cols, nb_r.at[step], *sems(step, NORM_B))
        norm_a = jnp.sum(na_r[step], axis=0)
        norm_b = jnp.sum(nb_r[step], axis=0)
        return (
            scaling / (norm_b * norm_c + epsilon),
            scaling / (norm_a * norm_c + epsilon),
            scaling / (norm_a * norm_b + epsilon),
        )

    def update_first(step, own_a, own_b, step_a, step_b):
        arrive(rows, rb.at[step], *sems(step, RS_B))
        arrive(cols, ra.at[step], *sems(step, RS_A))
        own_a = damping * own_a + step_a * jnp.sum(ra[step].astype(f32), axis=0)
        own_b = damping * own_b + step_b * jnp.sum(rb[step].astype(f32), axis=0)
        return own_a, own_b

    own_a, own_b = a_ref[...], b_ref[...]
    third16 = c_ref[...].astype(bf16)
    gram_c, norm_c = take_third(third16)
    cq[...] = c_ref[...].reshape(Q, 4, rank)
    own_c = cq[q]
    pl.semaphore_wait(barrier, N - 1 + Q - 1)
    gather_factors(0, own_a, own_b)

    def turn(i, carry):
        chunk(i).wait()
        swap(tv, tt, i * part, part)
        return carry

    lax.fori_loop(0, CHUNKS, turn, 0)

    take_factors(0)
    gram_a, gram_b = grams(0)
    do_first_modes(0, gram_a, gram_b, gram_c)
    send_norms(0)
    gc = third_mode(tt, ta32, tb16)
    scatter_third(0, gc, third16, split(gram_a * gram_b))
    step_a, step_b, step_c = sizes(0, norm_c)
    own_a, own_b = update_first(0, own_a, own_b, step_a, step_b)
    gather_factors(1, own_a, own_b)
    line_third(0)

    take_factors(1)
    gram_a, gram_b = grams(1)
    own_c = gather_third(0, own_c, step_c)
    gram_ab = split(gram_a * gram_b)
    gc = third_mode(tt, ta32, tb16)
    third16 = whole_third(0).astype(bf16)
    scatter_third(1, gc, third16, gram_ab)
    send_norms(1)
    gram_c, norm_c = take_third(third16)
    do_first_modes(1, gram_a, gram_b, gram_c)
    line_third(1)
    step_a, step_b, step_c = sizes(1, norm_c)
    own_a, own_b = update_first(1, own_a, own_b, step_a, step_b)
    oa_ref[...] = own_a
    ob_ref[...] = own_b
    gather_third(1, own_c, step_c)
    oc_ref[...] = whole_third(1)

    for group, dst, ss, rs in sent:
        others(group, dst, ss, rs).wait_send()


def hand_over(a_ref, b_ref, c_ref, oa_ref, ob_ref, oc_ref):
    oa_ref[...] = a_ref[...]
    ob_ref[...] = b_ref[...]
    oc_ref[...] = c_ref[...]


def local(tensor, factor_a, factor_b, factor_c):
    rows_i, rows_j, depth = tensor.shape
    mine_a, rank = factor_a.shape
    mine_b = factor_b.shape[0]
    vmem = pl.BlockSpec(memory_space=pltpu.VMEM)
    V, S, D = pltpu.VMEM, STEPS, pltpu.SemaphoreType.DMA
    outs = pl.pallas_call(
        kernel,
        out_shape=[jax.ShapeDtypeStruct(x.shape, f32) for x in (factor_a, factor_b, factor_c)],
        in_specs=[pl.BlockSpec(memory_space=pl.ANY), vmem, vmem, vmem],
        out_specs=[vmem, vmem, vmem],
        scratch_shapes=[
            V((rows_i, rows_j, depth), bf16),
            V((rows_i, depth, rows_j), bf16),
            V((S, N, mine_a, rank), bf16),
            V((S, N, mine_b, rank), bf16),
            V((rows_i, rank), f32),
            V((rows_j, rank), f32),
            V((rows_j, rank), bf16),
            V((depth, rank), bf16),
            V((Q, 4, rank), f32),
            V((rows_i, rank), f32),
            V((S, mine_a, rank), bf16),
            V((S, mine_b, rank), bf16),
            V((S, N, mine_a, rank), bf16),
            V((S, N, mine_b, rank), bf16),
            V((S, N, mine_a, rank), bf16),
            V((S, N, mine_b, rank), bf16),
            V((S, 1, rank), f32),
            V((S, 1, rank), f32),
            V((S, N, 1, rank), f32),
            V((S, N, 1, rank), f32),
            V((S, Q, 4, rank), f32),
            V((S, Q, 4, rank), f32),
            V((S, 4, rank), f32),
            V((S, Z, 4, rank), f32),
            V((S, 4, rank), f32),
            V((S, Q, 4, rank), f32),
            D((CHUNKS,)),
            D((6 * S,)),
            D((6 * S,)),
            D((2 * S,)),
            D((2 * S,)),
            D((S,)),
            D((S,)),
        ],
        compiler_params=pltpu.CompilerParams(collective_id=0, has_side_effects=True),
    )(tensor, factor_a, factor_b, factor_c)
    return pl.pallas_call(
        hand_over,
        out_shape=[jax.ShapeDtypeStruct(x.shape, f32) for x in (factor_a, factor_b, factor_c)],
        in_specs=[vmem, vmem, vmem],
        out_specs=[vmem, vmem, vmem],
    )(*outs)


def solution(mesh):
    return jax.shard_map(
        local,
        mesh=mesh,
        in_specs=(P("row", "col", None), P(("row", "col"), None), P(("col", "row"), None), P()),
        out_specs=(P(("row", "col"), None), P(("col", "row"), None), P()),
        check_vma=False,
    )
```

```python
import jax
import jax.numpy as jnp
from jax import lax
from jax.experimental import pallas as pl
from jax.experimental.pallas import tpu as pltpu
from jax.sharding import PartitionSpec as P

STEPS = 2
N = 16
Z = 8
Q = 32
damping = 0.9
scaling = 0.25
epsilon = 1e-06

MESH = pl.DeviceIdType.MESH
bf16, f32 = jnp.bfloat16, jnp.float32
UNROLL = 128
CHUNKS = 8


class Group:
    def __init__(self, size, me, device, ring, unit):
        self.size, self.me, self.device = size, me, device
        near = lambda d: min(d // unit % ring, -(d // unit) % ring)
        self.offsets = sorted(range(1, size), key=lambda d: -near(d))

    def each(self, act):
        for d in self.offsets:
            act(lax.rem(self.me + d, self.size))


def remote(group, peer, src, dst, ssem, rsem):
    return pltpu.make_async_remote_copy(
        src_ref=src, dst_ref=dst, send_sem=ssem, recv_sem=rsem, device_id=group.device(peer), device_id_type=MESH
    )


def split(g):
    hi = g.astype(bf16)
    return hi, (g - hi.astype(f32)).astype(bf16)


def split_dot(x16, parts):
    hi, lo = parts
    return jnp.dot(x16, hi, preferred_element_type=f32) + jnp.dot(x16, lo, preferred_element_type=f32)


def swap(tv, tt, base, count):
    for u in range(count):
        tt[base + u] = tv[base + u].T


def third_mode(tt, ta32, tb16):
    rows_i, depth, rows_j = tt.shape
    rank = ta32.shape[1]

    def body(ib, gc):
        block = tt[pl.ds(ib * UNROLL, UNROLL)].reshape(UNROLL * depth, rows_j)
        along = jnp.dot(block, tb16[...], preferred_element_type=f32)
        for u in range(UNROLL):
            gc = gc + along[u * depth : (u + 1) * depth] * ta32[pl.ds(ib * UNROLL + u, 1), :]
        return gc

    return lax.fori_loop(0, rows_i // UNROLL, body, jnp.zeros((depth, rank), f32))


def first_modes(tv, ta32, tb32, c16, ga):
    rows_i, rows_j, depth = tv.shape
    rank = c16.shape[1]

    def body(ib, gb):
        b = tb32[...]
        block = tv[pl.ds(ib * UNROLL, UNROLL)].reshape(UNROLL * rows_j, depth)
        along = jnp.dot(block, c16[...], preferred_element_type=f32)
        rows = []
        for u in range(UNROLL):
            z = along[u * rows_j : (u + 1) * rows_j]
            rows.append(jnp.sum(z * b, axis=0, keepdims=True))
            gb = gb + z * ta32[pl.ds(ib * UNROLL + u, 1), :]
        ga[pl.ds(ib * UNROLL, UNROLL), :] = jnp.concatenate(rows, axis=0)
        return gb

    return lax.fori_loop(0, rows_i // UNROLL, body, jnp.zeros((rows_j, rank), f32))


AG_A, AG_B, NORM_A, NORM_B, RS_A, RS_B = range(6)
PLANE_RS, PLANE_AG = range(2)


def kernel(
    t_ref, a_ref, b_ref, c_ref, oa_ref, ob_ref, oc_ref,
    tv, tt, ta, tb, ta32, tb32, tb16, c16, cq, ga,
    a16, b16, sa, sb, ra, rb, na_s, nb_s, na_r, nb_r, c1s, c1r, c2s, c2r, c3s, c3r,
    tsem, ssem, rsem, plane_ssem, plane_rsem, line_ssem, line_rsem,
):
    row, col = lax.axis_index("row"), lax.axis_index("col")
    x_lo, z = lax.div(row, Z), lax.rem(row, Z)
    q = x_lo * N + col
    rows_i, rows_j, depth = tv.shape
    rank = c16.shape[1]
    part = rows_i // CHUNKS
    rows = Group(N, row, lambda p: (p, col), Z, 1)
    cols = Group(N, col, lambda p: (row, p), 4, 2)
    plane = Group(Q, q, lambda p: (lax.div(p, N) * Z + z, lax.rem(p, N)), 4, 2)
    line = Group(Z, z, lambda p: (x_lo * Z + p, col), Z, 1)

    def chunk(i):
        view = pl.ds(i * part, part)
        return pltpu.make_async_copy(t_ref.at[view], tv.at[view], tsem.at[i])

    for i in range(CHUNKS):
        chunk(i).start()

    barrier = pltpu.get_barrier_semaphore()

    def greet(group):
        group.each(
            lambda p: pl.semaphore_signal(barrier, inc=1, device_id=group.device(p), device_id_type=MESH)
        )

    greet(rows)
    greet(plane)

    sent = []

    def others(group, dst, ss, rs):
        view = dst.at[pl.ds(0, group.size - 1)]
        return remote(group, group.me, view, view, ss, rs)

    def send(group, src_of, dst, ss, rs):
        group.each(lambda p: remote(group, p, src_of(p), dst.at[group.me], ss, rs).start())
        sent.append((group, dst, ss, rs))

    def arrive(group, dst, ss, rs):
        others(group, dst, ss, rs).wait_recv()

    def sems(step, kind):
        return ssem.at[step * 6 + kind], rsem.at[step * 6 + kind]

    def plane_sems(step, kind):
        return plane_ssem.at[step * 2 + kind], plane_rsem.at[step * 2 + kind]

    def line_sems(step):
        return line_ssem.at[step], line_rsem.at[step]

    def gather_factors(step, own_a, own_b):
        b16[step] = own_b.astype(bf16)
        a16[step] = own_a.astype(bf16)
        send(rows, lambda p: b16.at[step], tb.at[step], *sems(step, AG_B))
        send(cols, lambda p: a16.at[step], ta.at[step], *sems(step, AG_A))
        tb[step, row] = own_b.astype(bf16)
        ta[step, col] = own_a.astype(bf16)

    def take_third(third16):
        c16[...] = third16
        c32 = third16.astype(f32)
        gram = jnp.dot(c32.T.astype(bf16), third16, preferred_element_type=f32)
        return gram, jnp.sum(c32 * c32, axis=0, keepdims=True)

    def take_factors(step):
        arrive(cols, ta.at[step], *sems(step, AG_A))
        arrive(rows, tb.at[step], *sems(step, AG_B))
        a_full = ta[step].reshape(rows_i, rank).astype(f32)
        b_full = tb[step].astype(f32).reshape(rows_j, rank)
        ta32[...] = a_full
        tb32[...] = b_full
        tb16[...] = b_full.astype(bf16)

    def send_norms(step):
        a_full, b_full = ta32[...], tb32[...]
        part_na = jnp.sum(a_full * a_full, axis=0, keepdims=True)
        part_nb = jnp.sum(b_full * b_full, axis=0, keepdims=True)
        na_s[step] = part_na
        nb_s[step] = part_nb
        na_r[step, row] = part_na
        nb_r[step, col] = part_nb
        send(rows, lambda p: na_s.at[step], na_r.at[step], *sems(step, NORM_A))
        send(cols, lambda p: nb_s.at[step], nb_r.at[step], *sems(step, NORM_B))

    def grams(step):
        gram_a = jnp.dot(ta32[...].T.astype(bf16), ta[step].reshape(rows_i, rank), preferred_element_type=f32)
        gram_b = jnp.dot(tb32[...].T.astype(bf16), tb16[...], preferred_element_type=f32)
        return gram_a, gram_b

    def do_first_modes(step, gram_a, gram_b, gram_c):
        gb = first_modes(tv, ta32, tb32, c16, ga)
        gb = gb - split_dot(tb16[...], split(gram_a * gram_c))
        sb[step] = gb.reshape(N, 8, rank).astype(bf16)
        send(rows, lambda p: sb.at[step, p], rb.at[step], *sems(step, RS_B))
        grad_a = ga[...] - split_dot(ta[step].reshape(rows_i, rank), split(gram_b * gram_c))
        sa[step] = grad_a.astype(bf16).reshape(N, 16, rank)
        send(cols, lambda p: sa.at[step, p], ra.at[step], *sems(step, RS_A))
        rb[step, row] = sb[step, row]
        ra[step, col] = sa[step, col]

    def scatter_third(step, gc, third16, gram_ab):
        gc = gc - split_dot(third16, gram_ab)
        c1s[step] = gc.reshape(Q, 4, rank)
        send(plane, lambda p: c1s.at[step, p], c1r.at[step], *plane_sems(step, PLANE_RS))
        c1r[step, q] = c1s[step, q]

    def line_third(step):
        arrive(plane, c1r.at[step], *plane_sems(step, PLANE_RS))
        piece = jnp.sum(c1r[step], axis=0)
        c2s[step] = piece
        send(line, lambda p: c2s.at[step], c2r.at[step], *line_sems(step))
        c2r[step, z] = piece

    def gather_third(step, own_c, step_c):
        arrive(line, c2r.at[step], *line_sems(step))
        own_c = damping * own_c + step_c * jnp.sum(c2r[step], axis=0)
        c3s[step] = own_c
        send(plane, lambda p: c3s.at[step], c3r.at[step], *plane_sems(step, PLANE_AG))
        c3r[step, q] = own_c
        return own_c

    def whole_third(step):
        arrive(plane, c3r.at[step], *plane_sems(step, PLANE_AG))
        return c3r[step].reshape(depth, rank)

    def sizes(step, norm_c):
        arrive(rows, na_r.at[step], *sems(step, NORM_A))
        arrive(cols, nb_r.at[step], *sems(step, NORM_B))
        norm_a = jnp.sum(na_r[step], axis=0)
        norm_b = jnp.sum(nb_r[step], axis=0)
        return (
            scaling / (norm_b * norm_c + epsilon),
            scaling / (norm_a * norm_c + epsilon),
            scaling / (norm_a * norm_b + epsilon),
        )

    def update_first(step, own_a, own_b, step_a, step_b):
        arrive(rows, rb.at[step], *sems(step, RS_B))
        arrive(cols, ra.at[step], *sems(step, RS_A))
        own_a = damping * own_a + step_a * jnp.sum(ra[step].astype(f32), axis=0)
        own_b = damping * own_b + step_b * jnp.sum(rb[step].astype(f32), axis=0)
        return own_a, own_b

    own_a, own_b = a_ref[...], b_ref[...]
    third16 = c_ref[...].astype(bf16)
    gram_c, norm_c = take_third(third16)
    cq[...] = c_ref[...].reshape(Q, 4, rank)
    own_c = cq[q]
    pl.semaphore_wait(barrier, N - 1 + Q - 1)
    gather_factors(0, own_a, own_b)

    def turn(i, carry):
        chunk(i).wait()
        swap(tv, tt, i * part, part)
        return carry

    lax.fori_loop(0, CHUNKS, turn, 0)

    take_factors(0)
    gram_a, gram_b = grams(0)
    send_norms(0)
    do_first_modes(0, gram_a, gram_b, gram_c)
    gc = third_mode(tt, ta32, tb16)
    scatter_third(0, gc, third16, split(gram_a * gram_b))
    step_a, step_b, step_c = sizes(0, norm_c)
    own_a, own_b = update_first(0, own_a, own_b, step_a, step_b)
    gather_factors(1, own_a, own_b)
    line_third(0)

    take_factors(1)
    gram_a, gram_b = grams(1)
    own_c = gather_third(0, own_c, step_c)
    gram_ab = split(gram_a * gram_b)
    gc = third_mode(tt, ta32, tb16)
    third16 = whole_third(0).astype(bf16)
    scatter_third(1, gc, third16, gram_ab)
    send_norms(1)
    gram_c, norm_c = take_third(third16)
    do_first_modes(1, gram_a, gram_b, gram_c)
    line_third(1)
    step_a, step_b, step_c = sizes(1, norm_c)
    own_a, own_b = update_first(1, own_a, own_b, step_a, step_b)
    oa_ref[...] = own_a
    ob_ref[...] = own_b
    gather_third(1, own_c, step_c)
    oc_ref[...] = whole_third(1)

    for group, dst, ss, rs in sent:
        others(group, dst, ss, rs).wait_send()


def hand_over(a_ref, b_ref, c_ref, oa_ref, ob_ref, oc_ref):
    oa_ref[...] = a_ref[...]
    ob_ref[...] = b_ref[...]
    oc_ref[...] = c_ref[...]


def local(tensor, factor_a, factor_b, factor_c):
    rows_i, rows_j, depth = tensor.shape
    mine_a, rank = factor_a.shape
    mine_b = factor_b.shape[0]
    vmem = pl.BlockSpec(memory_space=pltpu.VMEM)
    V, S, D = pltpu.VMEM, STEPS, pltpu.SemaphoreType.DMA
    outs = pl.pallas_call(
        kernel,
        out_shape=[jax.ShapeDtypeStruct(x.shape, f32) for x in (factor_a, factor_b, factor_c)],
        in_specs=[pl.BlockSpec(memory_space=pl.ANY), vmem, vmem, vmem],
        out_specs=[vmem, vmem, vmem],
        scratch_shapes=[
            V((rows_i, rows_j, depth), bf16),
            V((rows_i, depth, rows_j), bf16),
            V((S, N, mine_a, rank), bf16),
            V((S, N, mine_b, rank), bf16),
            V((rows_i, rank), f32),
            V((rows_j, rank), f32),
            V((rows_j, rank), bf16),
            V((depth, rank), bf16),
            V((Q, 4, rank), f32),
            V((rows_i, rank), f32),
            V((S, mine_a, rank), bf16),
            V((S, mine_b, rank), bf16),
            V((S, N, mine_a, rank), bf16),
            V((S, N, mine_b, rank), bf16),
            V((S, N, mine_a, rank), bf16),
            V((S, N, mine_b, rank), bf16),
            V((S, 1, rank), f32),
            V((S, 1, rank), f32),
            V((S, N, 1, rank), f32),
            V((S, N, 1, rank), f32),
            V((S, Q, 4, rank), f32),
            V((S, Q, 4, rank), f32),
            V((S, 4, rank), f32),
            V((S, Z, 4, rank), f32),
            V((S, 4, rank), f32),
            V((S, Q, 4, rank), f32),
            D((CHUNKS,)),
            D((6 * S,)),
            D((6 * S,)),
            D((2 * S,)),
            D((2 * S,)),
            D((S,)),
            D((S,)),
        ],
        compiler_params=pltpu.CompilerParams(collective_id=0, has_side_effects=True),
    )(tensor, factor_a, factor_b, factor_c)
    return pl.pallas_call(
        hand_over,
        out_shape=[jax.ShapeDtypeStruct(x.shape, f32) for x in (factor_a, factor_b, factor_c)],
        in_specs=[vmem, vmem, vmem],
        out_specs=[vmem, vmem, vmem],
    )(*outs)


def solution(mesh):
    return jax.shard_map(
        local,
        mesh=mesh,
        in_specs=(P("row", "col", None), P(("row", "col"), None), P(("col", "row"), None), P()),
        out_specs=(P(("row", "col"), None), P(("col", "row"), None), P()),
        check_vma=False,
    )
```
